32 devices in a mesh: row: 4 (over y, x), col: 8 (over z, core).
Axes of the slice: x: 2, y: 2, z: 4, core: 2. Of those that a mesh axis runs over, the one named last changes fastest.
Arguments:
- fact_block: int32 [98304, 1], P(('row', 'col')), may hold values from 0 to 31; in each aligned block of 3072 rows (0 to 3071, 3072 to 6143, ...) at most 192 rows name the same one
- fact_offset: int32 [98304], P(('row', 'col')), may hold values from 0 to 2047
- fact_date: int32 [98304], P(('row', 'col')), may hold values from 0 to 2555
- revenue: bfloat16 [98304], P(('row', 'col')), may hold values from 0.5 to 4
- supplier_words: int32 [2208], P('col'), may hold values from 0 to 1073741823
- date_words: int32 [88], P('col'), may hold values from 0 to 1073741823
- candidates: int32 [1024], replicated, may hold values from 0 to 65535
Outputs:
- supplier_revenue: float32 [65536], P(('row', 'col'))
- candidate_revenue: float32 [1024], replicated
- candidate_total: float32 [], replicated
The draws below stay inside these ranges and needn't reach their ends.
Inputs may be any that keep to these rules, and one draw needn't show every extreme that they name: `fact_block`: each device's rows name no owner block more than 192 times. `candidates`: ids may repeat.
All inputs are finite; a program needn't handle non-finite values.
Results may differ from the reference program's by a relative error of at most 0.0003.
Values sent between devices are 32-bit elements; how exact they have to be, the bound alone decides.
A program may use at most 64 MiB of HBM per device.

```python
import math
import jax
import jax.numpy as jnp
import numpy as np

ROWS_DEV = 3072
SUP_DEV = 2048
DATES = 2556
CANDS = 1024
ROWS = 98304
SUPPLIERS = 65536
MASK_WORDS = 69
DATE_WORDS = 88
CAP = 192
DEVICES = 32


def with_ends(entries, stream_key, least, largest):
    spot = [jax.random.randint(jax.random.fold_in(stream_key, axis), (), 0, length) for axis, length in enumerate(entries.shape)]
    main_axis = entries.shape.index(max(entries.shape))
    beside = spot[:main_axis] + [(spot[main_axis] + 1) % entries.shape[main_axis]] + spot[main_axis + 1:]
    return entries.at[tuple(spot)].set(least).at[tuple(beside)].set(largest)


def shard_levels(rng, extent, pieces, least, top_value):
    gain, own = 1.0, jax.random.fold_in(rng, 6)
    for position, parts in pieces:
        draws = jnp.exp(jax.random.uniform(jax.random.fold_in(own, position), (parts,), jnp.float32, least / len(pieces), top_value / len(pieces)))
        gain = gain * jnp.repeat(draws, extent[position] // parts).reshape([-1 if axis == position else 1 for axis in range(len(extent))])
    return gain


def routed_block(stream_key, own, number, rows, amount, top, limit, skew):
    sequence = jax.random.permutation(stream_key, amount)
    heavy_load, usual = load_shares(amount, rows * top, limit, skew, True), load_shares(amount, rows * top, limit, skew, False)
    places = jnp.arange(amount)

    def named(lengths, offset_by):
        used = int((lengths > 0).sum())
        fixed = max(1, used // 4)
        moved = fixed + (places - fixed + offset_by * (used - fixed)) % max(1, amount - fixed)
        return jnp.zeros((amount,), jnp.int32).at[sequence[jnp.where(places < fixed, places, moved)]].set(jnp.asarray(lengths, jnp.int32))

    lengths = jnp.where(number % 4 == 0, named(heavy_load, number // 4), named(usual, number - number // 4 - 1))
    mixed = jax.random.permutation(jax.random.fold_in(own, 3), amount)
    giver, sink = mixed[0:amount // 2 * 2:2], mixed[1:amount // 2 * 2:2]
    margin = jnp.minimum(lengths[giver] - 1, limit - lengths[sink]) // 2
    margin = jnp.where((giver == sequence[0]) | (sink == sequence[0]) | (lengths[sink] == 0), 0, jnp.maximum(margin, 0))
    moved = jax.random.randint(jax.random.fold_in(own, 4), (amount // 2,), 0, 1 << 20) % (margin + 1)
    lengths = lengths.at[giver].add(-moved).at[sink].add(moved)
    items = jnp.searchsorted(jnp.cumsum(lengths), jnp.arange(rows * top), side="right").astype(jnp.int32)
    listing = items.reshape(top, rows).T
    listing = listing[jax.random.permutation(jax.random.fold_in(own, 1), rows)]
    offset_by = jax.random.randint(jax.random.fold_in(own, 2), (rows, 1), 0, top)
    return jnp.take_along_axis(listing, (jnp.arange(top)[None, :] + offset_by) % top, axis=1)


def load_shares(number_of, total, most, skew, full):
    portions = [(1 << 20) // math.isqrt(grade ** skew) + 1 for grade in range(1, number_of + 1)]
    largest = most if full else min(most, max(-(-total // number_of), total * portions[0] // sum(portions)))
    least = 1 if total - largest >= number_of - 1 else 0
    holding, surplus = [largest] + [least] * (number_of - 1), total - largest - least * (number_of - 1)
    while surplus > 0:
        movable = [i for i in range(1, number_of) if holding[i] < largest] or [i for i in range(1, number_of) if holding[i] < most]
        whole, left = sum([portions[i] for i in movable]), surplus
        for i in movable:
            addition = min(most - holding[i], max(1, left * portions[i] // whole), surplus)
            holding[i] = holding[i] + addition
            surplus = surplus - addition
    return np.array(holding)


def setup_inputs(seed: int = 0) -> dict:
    keys = jax.random.split(jax.random.key(seed), 8)
    fact_block_keys = jax.random.split(jax.random.fold_in(keys[0], 1), ROWS // ROWS_DEV)
    fact_block_turns = jax.random.permutation(jax.random.fold_in(keys[0], 3), ROWS // ROWS_DEV)
    fact_block = jax.vmap(lambda own, number: routed_block(jax.random.fold_in(keys[0], 2), own, number, ROWS_DEV, DEVICES, 1, CAP, 1))(fact_block_keys, fact_block_turns).reshape((ROWS, 1))
    fact_offset = with_ends(jax.random.randint(keys[1], (ROWS,), 0, SUP_DEV), jax.random.fold_in(keys[1], 1), 0, SUP_DEV - 1).astype(jnp.int32)
    fact_date = with_ends(jax.random.randint(keys[2], (ROWS,), 0, DATES), jax.random.fold_in(keys[2], 1), 0, DATES - 1).astype(jnp.int32)
    revenue = jnp.clip(jnp.exp(math.log(4.0) - 2.0794415 * jax.random.uniform(keys[3], (ROWS,), jnp.float32) ** shard_levels(keys[3], (ROWS,), ((0, 32),), -0.2, 0.2)), 0.5, 4.0).astype(jnp.bfloat16)
    supplier_words = with_ends(jax.random.randint(keys[4], (DEVICES * MASK_WORDS,), 0, 1073741824), jax.random.fold_in(keys[4], 1), 0, 1073741823).astype(jnp.int32)
    date_words = with_ends(jax.random.randint(keys[5], (DATE_WORDS,), 0, 1073741824), jax.random.fold_in(keys[5], 1), 0, 1073741823).astype(jnp.int32)
    candidates = with_ends(jax.random.randint(keys[6], (CANDS,), 0, SUPPLIERS), jax.random.fold_in(keys[6], 1), 0, SUPPLIERS - 1).astype(jnp.int32)
    return {"fact_block": fact_block, "fact_offset": fact_offset, "fact_date": fact_date, "revenue": revenue, "supplier_words": supplier_words, "date_words": date_words, "candidates": candidates}


def unpack(words, index, place):
    return jnp.bitwise_and(jnp.right_shift(words[index], place), 1)


def reference(fact_block, fact_offset, fact_date, revenue, supplier_words, date_words, candidates):
    owner = fact_block[:, 0]
    supplier_bit = unpack(supplier_words, (owner * MASK_WORDS + fact_offset // 30).astype(jnp.int32), (fact_offset % 30).astype(jnp.int32))
    date_bit = unpack(date_words, (fact_date // 30).astype(jnp.int32), (fact_date % 30).astype(jnp.int32))
    masked = jnp.where(supplier_bit * date_bit == 1, revenue, jnp.zeros_like(revenue))
    global_id = (owner * SUP_DEV + fact_offset).astype(jnp.int32)
    supplier_revenue = jax.ops.segment_sum(masked.astype(jnp.float32), global_id, num_segments=SUPPLIERS)
    candidate_revenue = supplier_revenue[candidates]
    candidate_total = jnp.sum(candidate_revenue)
    return supplier_revenue, candidate_revenue, candidate_total
```

```python
import functools

import jax
import jax.numpy as jnp
from jax import lax
from jax.experimental import pallas as pl
from jax.experimental.pallas import tpu as pltpu
from jax.sharding import PartitionSpec as P

SUP_DEV = 2048
LANES = 128
WIDE = 2 * LANES
GROUP = SUP_DEV // WIDE
BITS = 30
MESH = pl.DeviceIdType.MESH


def div_bits(x):
    return lax.shift_right_logical(x * 2185, 16)


def lookup(row, index):
    table = jnp.broadcast_to(row, index.shape)
    return jnp.take_along_axis(table, index, axis=1, mode="promise_in_bounds")


def kernel(
    rows_axis, cols_axis, date_words,
    block_ref, offset_ref, date_ref, rev_ref, cand_ref, sup_ref, dat_ref,
    owned_ref, cand_out_ref, total_ref,
    a_idx, b_idx, left, right, hist, dat_buf, sup_buf, part1, sum1, part2,
    cpart, cpart1, csum1, cpart2,
    dat_send, dat_recv, sup_send, sup_recv, h1_send, h1_recv, c1_send, c1_recv,
    h2_send, h2_recv, c2_send, c2_recv,
):
    R, C = rows_axis, cols_axis
    i, j = lax.axis_index("row"), lax.axis_index("col")
    row_peers = [(lax.rem(i + k, R), j) for k in range(1, R)]
    col_peers = [(i, lax.rem(j + k, C)) for k in range(1, C)]
    n_rows = block_ref.shape[0]
    chunks = hist.shape[0] // left.shape[0]
    tall = left.shape[0]

    barrier = pltpu.get_barrier_semaphore()
    for peer in col_peers + row_peers:
        pl.semaphore_signal(barrier, inc=1, device_id=peer, device_id_type=MESH)

    off = offset_ref[...]
    a_idx[...] = block_ref[...] * GROUP + (lax.shift_right_logical(off, 7) & (GROUP - 1))
    b_idx[...] = lax.shift_right_logical(off, 10) * LANES + (off & (LANES - 1))

    pl.semaphore_wait(barrier, (C - 1) + (R - 1))

    def remote(src, dst, send, recv, peer):
        return pltpu.make_async_remote_copy(
            src_ref=src, dst_ref=dst, send_sem=send, recv_sem=recv, device_id=peer, device_id_type=MESH
        )

    dat_copies = [
        remote(dat_ref, dat_buf.at[k], dat_send.at[k], dat_recv.at[k], col_peers[k]) for k in range(C - 1)
    ]
    sup_copies = [
        remote(sup_ref, sup_buf.at[k + 1], sup_send.at[k], sup_recv.at[k], col_peers[k]) for k in range(C - 1)
    ]
    for copy in dat_copies:
        copy.start()
    for copy in sup_copies:
        copy.start()

    iota_b = lax.broadcasted_iota(jnp.int32, (WIDE, LANES), 0)
    for r in range(n_rows):
        hit = iota_b == b_idx[r : r + 1, :]
        right[:, r * LANES : (r + 1) * LANES] = jnp.where(hit, 1.0, 0.0).astype(jnp.bfloat16)

    iota_a = lax.broadcasted_iota(jnp.int32, (tall, LANES), 0)
    rev = rev_ref[...].astype(jnp.float32)

    def build_left(base, values):
        for r in range(n_rows):
            hit = iota_a == a_idx[r : r + 1, :] - base
            left[:, r * LANES : (r + 1) * LANES] = jnp.where(hit, values[r : r + 1, :], 0.0).astype(jnp.bfloat16)

    day = date_ref[...]
    day_word = div_bits(day)
    day_bit = day - day_word * BITS

    for copy in dat_copies:
        copy.wait_recv()
    table = pltpu.roll(dat_ref[...], j * date_words, 1)
    for k in range(1, C):
        source = lax.rem(j - k + C, C)
        table = table + pltpu.roll(dat_buf[k - 1], source * date_words, 1)
    lit = lax.shift_right_logical(lookup(table, day_word), day_bit) & 1
    values = jnp.where(lit == 1, rev, 0.0)

    def histogram(base):
        build_left(base, values)
        return lax.dot_general(
            left[...], right[...], (((1,), (1,)), ((), ())), preferred_element_type=jnp.float32
        )

    if chunks == 1:
        hist[...] = histogram(0)
    else:

        def body(c, carry):
            base = pl.multiple_of(c * tall, tall)
            hist[pl.ds(base, tall), :] = histogram(base)
            return carry

        lax.fori_loop(0, chunks, body, 0)

    span = C * GROUP
    h1_copies = [
        remote(
            hist.at[pl.ds(pl.multiple_of(row_peers[k][0] * span, span), span), :],
            part1.at[k], h1_send.at[k], h1_recv.at[k], row_peers[k],
        )
        for k in range(R - 1)
    ]
    for copy in h1_copies:
        copy.start()

    cand = cand_ref[...]
    c_off = cand & (SUP_DEV - 1)
    c_owner = lax.div(cand, SUP_DEV) if SUP_DEV & (SUP_DEV - 1) else lax.shift_right_logical(cand, 11)
    c_row = c_owner * GROUP + (lax.shift_right_logical(c_off, 7) & (GROUP - 1))
    c_high = c_off >= SUP_DEV // 2
    c_lane = c_off & (LANES - 1)

    def pick(g, acc):
        base = pl.multiple_of(g * 8, 8)
        tile = hist[pl.ds(base, 8), :]
        for s in range(8):
            low = lookup(tile[s : s + 1, :LANES], c_lane)
            high = lookup(tile[s : s + 1, LANES:], c_lane)
            acc = jnp.where(c_row == base + s, jnp.where(c_high, high, low), acc)
        return acc

    picked = lax.fori_loop(0, hist.shape[0] // 8, pick, jnp.zeros(cand.shape, jnp.float32))
    cpart[...] = picked
    cpart1[i] = picked
    c1_copies = [
        remote(cpart, cpart1.at[i], c1_send.at[k], c1_recv.at[k], row_peers[k]) for k in range(R - 1)
    ]
    for copy in c1_copies:
        copy.start()

    sup_buf[0] = sup_ref[...]
    for copy in sup_copies:
        copy.wait_recv()
    c_word = div_bits(c_off)
    c_bit = c_off - c_word * BITS

    def word_of(k, acc):
        source = lax.rem(j - k + C, C)
        for r in range(R):
            word = lookup(sup_buf[k, r : r + 1, :], c_word)
            acc = jnp.where(c_owner == source * R + r, word, acc)
        return acc

    c_words = lax.fori_loop(0, C, word_of, jnp.zeros(cand.shape, jnp.int32))
    c_lit = (lax.shift_right_logical(c_words, c_bit) & 1) == 1

    me = i * C + j
    holder = me // R
    slot = lax.rem(j - holder + C, C)
    my_words = sup_buf[slot, pl.ds(lax.rem(me, R), 1), :]
    spot = lax.broadcasted_iota(jnp.int32, owned_ref.shape, 0) * LANES + lax.broadcasted_iota(
        jnp.int32, owned_ref.shape, 1
    )
    spot_word = div_bits(spot)
    my_lit = (lax.shift_right_logical(lookup(my_words, spot_word), spot - spot_word * BITS) & 1) == 1

    for copy in h1_copies:
        copy.wait_recv()
    total = hist[pl.ds(pl.multiple_of(i * span, span), span), :]
    for k in range(R - 1):
        total = total + part1[k]
    sum1[...] = total
    h2_copies = [
        remote(
            sum1.at[pl.ds(pl.multiple_of(col_peers[k][1] * GROUP, GROUP), GROUP), :],
            part2.at[k], h2_send.at[k], h2_recv.at[k], col_peers[k],
        )
        for k in range(C - 1)
    ]
    for copy in h2_copies:
        copy.start()
    for copy in c1_copies:
        copy.wait_recv()
    ctotal = cpart1[0]
    for k in range(1, R):
        ctotal = ctotal + cpart1[k]
    csum1[...] = ctotal
    cpart2[j] = ctotal
    c2_copies = [
        remote(csum1, cpart2.at[j], c2_send.at[k], c2_recv.at[k], col_peers[k]) for k in range(C - 1)
    ]
    for copy in c2_copies:
        copy.start()

    for copy in h2_copies:
        copy.wait_recv()
    mine = sum1[pl.ds(pl.multiple_of(j * GROUP, GROUP), GROUP), :]
    for k in range(C - 1):
        mine = mine + part2[k]
    owned_ref[:GROUP, :] = jnp.where(my_lit[:GROUP], mine[:, :LANES], 0.0)
    owned_ref[GROUP:, :] = jnp.where(my_lit[GROUP:], mine[:, LANES:], 0.0)

    for copy in c2_copies:
        copy.wait_recv()
    ctotal = cpart2[0]
    for k in range(1, C):
        ctotal = ctotal + cpart2[k]
    result = jnp.where(c_lit, ctotal, 0.0)
    cand_out_ref[...] = result
    total_ref[0, 0] = jnp.sum(result)

    for copy in dat_copies + sup_copies + h1_copies + c1_copies + h2_copies + c2_copies:
        copy.wait_send()


def per_device(R, C, fact_block, fact_offset, fact_date, revenue, supplier_words, date_words, candidates):
    rows = fact_offset.shape[0] // LANES
    cands = candidates.shape[0] // LANES
    n_dates = date_words.shape[0]
    per_block = supplier_words.shape[0] // R
    tall_all = R * C * GROUP
    tall = min(tall_all, WIDE)
    words = jnp.pad(supplier_words.reshape(R, per_block), ((0, 0), (0, LANES - per_block)))
    dates = jnp.pad(date_words.reshape(1, n_dates), ((0, 0), (0, LANES - n_dates)))
    span = C * GROUP
    f32, i32 = jnp.float32, jnp.int32
    dma = pltpu.SemaphoreType.DMA
    vmem = pl.BlockSpec(memory_space=pltpu.VMEM)
    owned, cand_rev, total = pl.pallas_call(
        functools.partial(kernel, R, C, n_dates),
        out_shape=(
            jax.ShapeDtypeStruct((SUP_DEV // LANES, LANES), f32),
            jax.ShapeDtypeStruct((cands, LANES), f32),
            jax.ShapeDtypeStruct((1, 1), f32),
        ),
        in_specs=[vmem] * 7,
        out_specs=(vmem, vmem, pl.BlockSpec(memory_space=pltpu.SMEM)),
        scratch_shapes=[
            pltpu.VMEM((rows, LANES), i32),
            pltpu.VMEM((rows, LANES), i32),
            pltpu.VMEM((tall, rows * LANES), jnp.bfloat16),
            pltpu.VMEM((WIDE, rows * LANES), jnp.bfloat16),
            pltpu.VMEM((tall_all, WIDE), f32),
            pltpu.VMEM((C - 1, 1, LANES), i32),
            pltpu.VMEM((C, R, LANES), i32),
            pltpu.VMEM((R - 1, span, WIDE), f32),
            pltpu.VMEM((span, WIDE), f32),
            pltpu.VMEM((C - 1, GROUP, WIDE), f32),
            pltpu.VMEM((cands, LANES), f32),
            pltpu.VMEM((R, cands, LANES), f32),
            pltpu.VMEM((cands, LANES), f32),
            pltpu.VMEM((C, cands, LANES), f32),
            dma((C - 1,)), dma((C - 1,)), dma((C - 1,)), dma((C - 1,)),
            dma((R - 1,)), dma((R - 1,)), dma((R - 1,)), dma((R - 1,)),
            dma((C - 1,)), dma((C - 1,)), dma((C - 1,)), dma((C - 1,)),
        ],
        compiler_params=pltpu.CompilerParams(collective_id=0, has_side_effects=True),
        name="revenue",
    )(
        fact_block.reshape(rows, LANES),
        fact_offset.reshape(rows, LANES),
        fact_date.reshape(rows, LANES),
        revenue.reshape(rows, LANES),
        candidates.reshape(cands, LANES),
        words,
        dates,
    )
    return owned.reshape(SUP_DEV), cand_rev.reshape(candidates.shape), total.reshape(())


def solution(mesh):
    in_specs = (
        P(("row", "col"), None),
        P(("row", "col")),
        P(("row", "col")),
        P(("row", "col")),
        P("col"),
        P("col"),
        P(),
    )
    out_specs = (P(("row", "col")), P(), P())
    body = functools.partial(per_device, mesh.shape["row"], mesh.shape["col"])
    return jax.shard_map(body, mesh=mesh, in_specs=in_specs, out_specs=out_specs, check_vma=False)
```

```python
import functools

import jax
import jax.numpy as jnp
from jax import lax
from jax.experimental import pallas as pl
from jax.experimental.pallas import tpu as pltpu
from jax.sharding import PartitionSpec as P

SUP_DEV = 2048
LANES = 128
WIDE = 2 * LANES
GROUP = SUP_DEV // WIDE
BITS = 30
MESH = pl.DeviceIdType.MESH


def div_bits(x):
    return lax.shift_right_logical(x * 2185, 16)


def lookup(row, index):
    table = jnp.broadcast_to(row, index.shape)
    return jnp.take_along_axis(table, index, axis=1, mode="promise_in_bounds")


def kernel(
    rows_axis, cols_axis,
    block_in, offset_in, date_in, rev_in, cand_in, sup_in, dat_in,
    both_ref, total_ref,
    block_ref, offset_ref, date_ref, rev_ref, cand_ref, load_sem, dat_row,
    a_idx, b_idx, left, right, hist, dat_buf, sup_buf, part1, sum1, part2,
    cpart, cpart1, csum1, cpart2,
    dat_send, dat_recv, sup_send, sup_recv, h1_send, h1_recv, c1_send, c1_recv,
    h2_send, h2_recv, c2_send, c2_recv,
):
    R, C = rows_axis, cols_axis
    i, j = lax.axis_index("row"), lax.axis_index("col")
    row_peers = [(lax.rem(i + k, R), j) for k in range(1, R)]
    col_peers = [(i, lax.rem(j + k, C)) for k in range(1, C)]
    n_rows = block_ref.shape[0]
    n_dates, n_words = dat_in.shape[1], sup_in.shape[0]
    per_block = n_words // R
    owned_rows = both_ref.shape[0] - cand_ref.shape[0]
    chunks = hist.shape[0] // left.shape[0]
    tall = left.shape[0]

    barrier = pltpu.get_barrier_semaphore()
    for peer in col_peers + row_peers:
        pl.semaphore_signal(barrier, inc=1, device_id=peer, device_id_type=MESH)

    pairs = [
        (offset_in, offset_ref), (block_in, block_ref), (date_in, date_ref), (rev_in, rev_ref),
        (cand_in, cand_ref), (dat_in, dat_buf.at[j]), (sup_in, sup_buf.at[j, 0]),
    ]
    loads = [pltpu.make_async_copy(src, dst, load_sem.at[n]) for n, (src, dst) in enumerate(pairs)]
    for load in loads:
        load.start()
    dat_row[...] = jnp.zeros_like(dat_row)
    for load in loads:
        load.wait()

    off = offset_ref[...]
    a_idx[...] = block_ref[...] * GROUP + (lax.shift_right_logical(off, 7) & (GROUP - 1))
    b_idx[...] = lax.shift_right_logical(off, 10) * LANES + (off & (LANES - 1))

    pl.semaphore_wait(barrier, (C - 1) + (R - 1))

    def remote(src, dst, send, recv, peer):
        return pltpu.make_async_remote_copy(
            src_ref=src, dst_ref=dst, send_sem=send, recv_sem=recv, device_id=peer, device_id_type=MESH
        )

    dat_copies = [
        remote(dat_in, dat_buf.at[j], dat_send.at[k], dat_recv.at[k], col_peers[k]) for k in range(C - 1)
    ]
    sup_copies = [
        remote(sup_in, sup_buf.at[j, 0], sup_send.at[k], sup_recv.at[k], col_peers[k]) for k in range(C - 1)
    ]
    for copy in dat_copies:
        copy.start()
    for copy in sup_copies:
        copy.start()

    iota_b = lax.broadcasted_iota(jnp.int32, (WIDE, LANES), 0)
    for r in range(n_rows):
        hit = iota_b == b_idx[r : r + 1, :]
        right[:, r * LANES : (r + 1) * LANES] = jnp.where(hit, 1.0, 0.0).astype(jnp.bfloat16)

    iota_a = lax.broadcasted_iota(jnp.int32, (tall, LANES), 0)
    rev = rev_ref[...].astype(jnp.float32)

    def build_left(base, values):
        for r in range(n_rows):
            hit = iota_a == a_idx[r : r + 1, :] - base
            left[:, r * LANES : (r + 1) * LANES] = jnp.where(hit, values[r : r + 1, :], 0.0).astype(jnp.bfloat16)

    day = date_ref[...]
    day_word = div_bits(day)
    day_bit = day - day_word * BITS

    for copy in dat_copies:
        copy.wait_recv()
    for c in range(C):
        dat_row[:, c * n_dates : (c + 1) * n_dates] = dat_buf[c]
    table = dat_row[...]
    lit = lax.shift_right_logical(lookup(table, day_word), day_bit) & 1
    values = jnp.where(lit == 1, rev, 0.0)

    def histogram(base):
        build_left(base, values)
        return lax.dot_general(
            left[...], right[...], (((1,), (1,)), ((), ())), preferred_element_type=jnp.float32
        )

    if chunks == 1:
        hist[...] = histogram(0)
    else:

        def body(c, carry):
            base = pl.multiple_of(c * tall, tall)
            hist[pl.ds(base, tall), :] = histogram(base)
            return carry

        lax.fori_loop(0, chunks, body, 0)

    span = C * GROUP
    h1_copies = [
        remote(
            hist.at[pl.ds(pl.multiple_of(row_peers[k][0] * span, span), span), :],
            part1.at[k], h1_send.at[k], h1_recv.at[k], row_peers[k],
        )
        for k in range(R - 1)
    ]
    for copy in h1_copies:
        copy.start()

    cand = cand_ref[...]
    c_off = cand & (SUP_DEV - 1)
    c_owner = lax.div(cand, SUP_DEV) if SUP_DEV & (SUP_DEV - 1) else lax.shift_right_logical(cand, 11)
    c_row = c_owner * GROUP + (lax.shift_right_logical(c_off, 7) & (GROUP - 1))
    c_high = c_off >= SUP_DEV // 2
    c_lane = c_off & (LANES - 1)

    def pick(g, acc):
        base = pl.multiple_of(g * 8, 8)
        tile = hist[pl.ds(base, 8), :]
        for s in range(8):
            low = lookup(tile[s : s + 1, :LANES], c_lane)
            high = lookup(tile[s : s + 1, LANES:], c_lane)
            acc = jnp.where(c_row == base + s, jnp.where(c_high, high, low), acc)
        return acc

    picked = lax.fori_loop(0, hist.shape[0] // 8, pick, jnp.zeros(cand.shape, jnp.float32))
    cpart[...] = picked
    cpart1[i] = picked
    c1_copies = [
        remote(cpart, cpart1.at[i], c1_send.at[k], c1_recv.at[k], row_peers[k]) for k in range(R - 1)
    ]
    for copy in c1_copies:
        copy.start()

    for copy in sup_copies:
        copy.wait_recv()

    full = n_words // LANES

    def words_at(source, flat):
        word = lookup(sup_buf[source, :, n_words - LANES :], jnp.maximum(flat - (n_words - LANES), 0))
        for t in range(full):
            near = (flat >= t * LANES) & (flat < (t + 1) * LANES)
            word = jnp.where(near, lookup(sup_buf[source, :, t * LANES : (t + 1) * LANES], flat & (LANES - 1)), word)
        return word

    c_word = div_bits(c_off)
    c_bit = c_off - c_word * BITS
    c_col = lax.div(c_owner, R)
    c_flat = (c_owner - c_col * R) * per_block + c_word

    def word_of(source, acc):
        return jnp.where(c_col == source, words_at(source, c_flat), acc)

    c_words = lax.fori_loop(0, C, word_of, jnp.zeros(cand.shape, jnp.int32))
    c_lit = (lax.shift_right_logical(c_words, c_bit) & 1) == 1

    me = i * C + j
    shape = (owned_rows, LANES)
    spot = lax.broadcasted_iota(jnp.int32, shape, 0) * LANES + lax.broadcasted_iota(jnp.int32, shape, 1)
    spot_word = div_bits(spot)
    my_words = words_at(me // R, lax.rem(me, R) * per_block + spot_word)
    my_lit = (lax.shift_right_logical(my_words, spot - spot_word * BITS) & 1) == 1

    for copy in h1_copies:
        copy.wait_recv()
    total = hist[pl.ds(pl.multiple_of(i * span, span), span), :]
    for k in range(R - 1):
        total = total + part1[k]
    sum1[...] = total
    h2_copies = [
        remote(
            sum1.at[pl.ds(pl.multiple_of(col_peers[k][1] * GROUP, GROUP), GROUP), :],
            part2.at[k], h2_send.at[k], h2_recv.at[k], col_peers[k],
        )
        for k in range(C - 1)
    ]
    for copy in h2_copies:
        copy.start()
    for copy in c1_copies:
        copy.wait_recv()
    ctotal = cpart1[0]
    for k in range(1, R):
        ctotal = ctotal + cpart1[k]
    csum1[...] = ctotal
    cpart2[j] = ctotal
    c2_copies = [
        remote(csum1, cpart2.at[j], c2_send.at[k], c2_recv.at[k], col_peers[k]) for k in range(C - 1)
    ]
    for copy in c2_copies:
        copy.start()

    for copy in h2_copies:
        copy.wait_recv()
    mine = sum1[pl.ds(pl.multiple_of(j * GROUP, GROUP), GROUP), :]
    for k in range(C - 1):
        mine = mine + part2[k]
    both_ref[:GROUP, :] = jnp.where(my_lit[:GROUP], mine[:, :LANES], 0.0)
    both_ref[GROUP:owned_rows, :] = jnp.where(my_lit[GROUP:], mine[:, LANES:], 0.0)

    for copy in c2_copies:
        copy.wait_recv()
    ctotal = cpart2[0]
    for k in range(1, C):
        ctotal = ctotal + cpart2[k]
    result = jnp.where(c_lit, ctotal, 0.0)
    both_ref[owned_rows:, :] = result
    total_ref[0, 0] = jnp.sum(result)

    for copy in dat_copies + sup_copies + h1_copies + c1_copies + h2_copies + c2_copies:
        copy.wait_send()


def per_device(R, C, fact_block, fact_offset, fact_date, revenue, supplier_words, date_words, candidates):
    rows = fact_offset.shape[0] // LANES
    cands = candidates.shape[0] // LANES
    tall_all = R * C * GROUP
    tall = min(tall_all, WIDE)
    span = C * GROUP
    f32, i32 = jnp.float32, jnp.int32
    dma = pltpu.SemaphoreType.DMA
    vmem = pl.BlockSpec(memory_space=pltpu.VMEM)
    both, total = pl.pallas_call(
        functools.partial(kernel, R, C),
        out_shape=(
            jax.ShapeDtypeStruct((SUP_DEV // LANES + cands, LANES), f32),
            jax.ShapeDtypeStruct((1, 1), f32),
        ),
        in_specs=[pl.BlockSpec(memory_space=pl.ANY)] * 7,
        out_specs=(vmem, pl.BlockSpec(memory_space=pltpu.SMEM)),
        scratch_shapes=[
            pltpu.VMEM((rows, LANES), i32),
            pltpu.VMEM((rows, LANES), i32),
            pltpu.VMEM((rows, LANES), i32),
            pltpu.VMEM((rows, LANES), revenue.dtype),
            pltpu.VMEM((cands, LANES), i32),
            dma((7,)),
            pltpu.VMEM((1, LANES), i32),
            pltpu.VMEM((rows, LANES), i32),
            pltpu.VMEM((rows, LANES), i32),
            pltpu.VMEM((tall, rows * LANES), jnp.bfloat16),
            pltpu.VMEM((WIDE, rows * LANES), jnp.bfloat16),
            pltpu.VMEM((tall_all, WIDE), f32),
            pltpu.VMEM((C, 1, date_words.shape[0]), i32),
            pltpu.VMEM((C, 1, supplier_words.shape[0]), i32),
            pltpu.VMEM((R - 1, span, WIDE), f32),
            pltpu.VMEM((span, WIDE), f32),
            pltpu.VMEM((C - 1, GROUP, WIDE), f32),
            pltpu.VMEM((cands, LANES), f32),
            pltpu.VMEM((R, cands, LANES), f32),
            pltpu.VMEM((cands, LANES), f32),
            pltpu.VMEM((C, cands, LANES), f32),
            dma((C - 1,)), dma((C - 1,)), dma((C - 1,)), dma((C - 1,)),
            dma((R - 1,)), dma((R - 1,)), dma((R - 1,)), dma((R - 1,)),
            dma((C - 1,)), dma((C - 1,)), dma((C - 1,)), dma((C - 1,)),
        ],
        compiler_params=pltpu.CompilerParams(collective_id=0, has_side_effects=True),
        name="revenue",
    )(
        fact_block.reshape(rows, LANES),
        fact_offset.reshape(rows, LANES),
        fact_date.reshape(rows, LANES),
        revenue.reshape(rows, LANES),
        candidates.reshape(cands, LANES),
        supplier_words,
        date_words.reshape(1, -1),
    )
    owned = both[: SUP_DEV // LANES].reshape(SUP_DEV)
    return owned, both[SUP_DEV // LANES :].reshape(candidates.shape), total.reshape(())


def solution(mesh):
    in_specs = (
        P(("row", "col"), None),
        P(("row", "col")),
        P(("row", "col")),
        P(("row", "col")),
        P("col"),
        P("col"),
        P(),
    )
    out_specs = (P(("row", "col")), P(), P())
    body = functools.partial(per_device, mesh.shape["row"], mesh.shape["col"])
    return jax.shard_map(body, mesh=mesh, in_specs=in_specs, out_specs=out_specs, check_vma=False)
```

```python
import functools

import jax
import jax.numpy as jnp
from jax import lax
from jax.experimental import pallas as pl
from jax.experimental.pallas import tpu as pltpu
from jax.sharding import PartitionSpec as P

SUP_DEV = 2048
LANES = 128
WIDE = 2 * LANES
GROUP = SUP_DEV // WIDE
BITS = 30
MESH = pl.DeviceIdType.MESH


def div_bits(x):
    return lax.shift_right_logical(x * 2185, 16)


def lookup(row, index):
    table = jnp.broadcast_to(row, index.shape)
    return jnp.take_along_axis(table, index, axis=1, mode="promise_in_bounds")


def kernel(
    rows_axis, cols_axis,
    block_in, offset_in, date_in, rev_in, cand_in, sup_in, dat_in,
    both_ref, total_ref,
    block_ref, offset_ref, date_ref, rev_ref, cand_ref, load_sem, dat_row,
    ids, rev32, a_idx, b_idx, left, right, low_left, c_hot, dat_buf, sup_buf,
    peer_ids, peer_dates, peer_revs, sum1, part2,
    cpart, cpart1, csum1, cpart2,
    dat_send, dat_recv, sup_send, sup_recv, row_send, row_recv, c1_send, c1_recv,
    h2_send, h2_recv, c2_send, c2_recv,
):
    R, C = rows_axis, cols_axis
    i, j = lax.axis_index("row"), lax.axis_index("col")
    row_peers = [(lax.rem(i + k, R), j) for k in range(1, R)]
    col_peers = [(i, lax.rem(j + k, C)) for k in range(1, C)]
    n_rows = block_ref.shape[0]
    n_dates, n_words = dat_in.shape[1], sup_in.shape[0]
    per_block = n_words // R
    owned_rows = both_ref.shape[0] - cand_ref.shape[0]
    chunks = R * C * GROUP // left.shape[0]
    tall = left.shape[0]

    barrier = pltpu.get_barrier_semaphore()
    for peer in col_peers + row_peers:
        pl.semaphore_signal(barrier, inc=1, device_id=peer, device_id_type=MESH)

    pairs = [
        (offset_in, offset_ref), (block_in, block_ref), (date_in, date_ref), (rev_in, rev_ref),
        (cand_in, cand_ref), (dat_in, dat_buf.at[j]), (sup_in, sup_buf.at[j, 0]),
    ]
    loads = [pltpu.make_async_copy(src, dst, load_sem.at[n]) for n, (src, dst) in enumerate(pairs)]
    for load in loads:
        load.start()
    dat_row[...] = jnp.zeros_like(dat_row)
    for load in loads:
        load.wait()

    off = offset_ref[...]
    rev = rev_ref[...].astype(jnp.float32)
    ids[...] = block_ref[...] * SUP_DEV + off
    rev32[...] = rev
    a_idx[...] = block_ref[...] * GROUP + (lax.shift_right_logical(off, 7) & (GROUP - 1))
    b_idx[...] = lax.shift_right_logical(off, 10) * LANES + (off & (LANES - 1))

    pl.semaphore_wait(barrier, (C - 1) + (R - 1))

    def remote(src, dst, send, recv, peer):
        return pltpu.make_async_remote_copy(
            src_ref=src, dst_ref=dst, send_sem=send, recv_sem=recv, device_id=peer, device_id_type=MESH
        )

    dat_copies = [
        remote(dat_in, dat_buf.at[j], dat_send.at[k], dat_recv.at[k], col_peers[k]) for k in range(C - 1)
    ]
    sup_copies = [
        remote(sup_in, sup_buf.at[j, 0], sup_send.at[k], sup_recv.at[k], col_peers[k]) for k in range(C - 1)
    ]
    for copy in dat_copies:
        copy.start()
    row_copies = [
        [
            remote(src, dst.at[k], row_send.at[n, k], row_recv.at[n, k], row_peers[k])
            for n, (src, dst) in enumerate(((ids, peer_ids), (date_ref, peer_dates), (rev32, peer_revs)))
        ]
        for k in range(R - 1)
    ]
    for copies in row_copies:
        for copy in copies:
            copy.start()
    for copy in sup_copies:
        copy.start()

    iota_b = lax.broadcasted_iota(jnp.int32, (WIDE, LANES), 0)

    def build_right(columns):
        for r in range(n_rows):
            hit = iota_b == columns[r : r + 1, :]
            right[:, r * LANES : (r + 1) * LANES] = jnp.where(hit, 1.0, 0.0).astype(jnp.bfloat16)

    def build_left(where, lines, values):
        iota_a = lax.broadcasted_iota(jnp.int32, (where.shape[0], LANES), 0)
        for r in range(n_rows):
            hit = iota_a == lines[r : r + 1, :]
            where[:, r * LANES : (r + 1) * LANES] = jnp.where(hit, values[r : r + 1, :], 0.0).astype(jnp.bfloat16)

    def product(lines, columns):
        return lax.dot_general(lines, columns, (((1,), (1,)), ((), ())), preferred_element_type=jnp.float32)

    cand = cand_ref[...]
    c_owner = lax.shift_right_logical(cand, 11)
    c_off = cand & (SUP_DEV - 1)
    c_row = c_owner * GROUP + (lax.shift_right_logical(c_off, 7) & (GROUP - 1))
    c_col = lax.shift_right_logical(c_off, 10) * LANES + (c_off & (LANES - 1))
    groups = cand.shape[0]

    def build_hot(base):
        iota_c = lax.broadcasted_iota(jnp.int32, (tall, LANES), 0)
        for g in range(groups):
            hit = iota_c == c_row[g : g + 1, :] - base
            c_hot[:, g * LANES : (g + 1) * LANES] = jnp.where(hit, 1.0, 0.0).astype(jnp.bfloat16)

    if chunks == 1:
        build_hot(0)

    build_right(b_idx[...])

    for copy in dat_copies:
        copy.wait_recv()
    for c in range(C):
        dat_row[:, c * n_dates : (c + 1) * n_dates] = dat_buf[c]
    table = dat_row[...]

    def dated(day, values):
        day_word = div_bits(day)
        lit = lax.shift_right_logical(lookup(table, day_word), day - day_word * BITS) & 1
        return jnp.where(lit == 1, values, 0.0)

    values = dated(date_ref[...], rev)

    def candidate_columns(base):
        build_left(left, a_idx[...] - base, values)
        rest = product(right[...], left[...])
        found = jnp.zeros((WIDE, groups * LANES), jnp.float32)
        for _ in range(3):
            term = rest.astype(jnp.bfloat16)
            rest = rest - term.astype(jnp.float32)
            found = found + jnp.dot(term, c_hot[...], preferred_element_type=jnp.float32)
        return found

    if chunks == 1:
        found = candidate_columns(0)
    else:

        def body(c, acc):
            build_hot(c * tall)
            return acc + candidate_columns(c * tall)

        found = lax.fori_loop(0, chunks, body, jnp.zeros((WIDE, groups * LANES), jnp.float32))
    picked = []
    for g in range(groups):
        hit = iota_b == c_col[g : g + 1, :]
        picked.append(jnp.sum(jnp.where(hit, found[:, g * LANES : (g + 1) * LANES], 0.0), axis=0, keepdims=True))
    picked = jnp.concatenate(picked, axis=0)
    cpart[...] = picked
    cpart1[i] = picked
    c1_copies = [
        remote(cpart, cpart1.at[i], c1_send.at[k], c1_recv.at[k], row_peers[k]) for k in range(R - 1)
    ]
    for copy in c1_copies:
        copy.start()

    span = C * GROUP
    build_left(low_left, a_idx[...] - i * span, values)
    total = product(low_left[...], right[...])
    for k in range(R - 1):
        for copy in row_copies[k]:
            copy.wait_recv()
        peer_id = peer_ids[k]
        line = lax.shift_right_logical(peer_id, 11) * GROUP + (lax.shift_right_logical(peer_id, 7) & (GROUP - 1))
        build_right((lax.shift_right_logical(peer_id, 10) & 1) * LANES + (peer_id & (LANES - 1)))
        build_left(low_left, line - i * span, dated(peer_dates[k], peer_revs[k]))
        total = total + product(low_left[...], right[...])
    sum1[...] = total
    h2_copies = [
        remote(
            sum1.at[pl.ds(pl.multiple_of(col_peers[k][1] * GROUP, GROUP), GROUP), :],
            part2.at[k], h2_send.at[k], h2_recv.at[k], col_peers[k],
        )
        for k in range(C - 1)
    ]
    for copy in h2_copies:
        copy.start()

    for copy in c1_copies:
        copy.wait_recv()
    ctotal = cpart1[0]
    for k in range(1, R):
        ctotal = ctotal + cpart1[k]
    csum1[...] = ctotal
    cpart2[j] = ctotal
    c2_copies = [
        remote(csum1, cpart2.at[j], c2_send.at[k], c2_recv.at[k], col_peers[k]) for k in range(C - 1)
    ]
    for copy in c2_copies:
        copy.start()

    for copy in sup_copies:
        copy.wait_recv()

    full = n_words // LANES

    def words_at(source, flat):
        word = lookup(sup_buf[source, :, n_words - LANES :], jnp.maximum(flat - (n_words - LANES), 0))
        for t in range(full):
            near = (flat >= t * LANES) & (flat < (t + 1) * LANES)
            word = jnp.where(near, lookup(sup_buf[source, :, t * LANES : (t + 1) * LANES], flat & (LANES - 1)), word)
        return word

    c_word = div_bits(c_off)
    c_bit = c_off - c_word * BITS
    c_source = lax.div(c_owner, R)
    c_flat = (c_owner - c_source * R) * per_block + c_word

    def word_of(source, acc):
        return jnp.where(c_source == source, words_at(source, c_flat), acc)

    c_words = lax.fori_loop(0, C, word_of, jnp.zeros(cand.shape, jnp.int32))
    c_lit = (lax.shift_right_logical(c_words, c_bit) & 1) == 1

    me = i * C + j
    shape = (owned_rows, LANES)
    spot = lax.broadcasted_iota(jnp.int32, shape, 0) * LANES + lax.broadcasted_iota(jnp.int32, shape, 1)
    spot_word = div_bits(spot)
    my_words = words_at(me // R, lax.rem(me, R) * per_block + spot_word)
    my_lit = (lax.shift_right_logical(my_words, spot - spot_word * BITS) & 1) == 1

    for copy in h2_copies:
        copy.wait_recv()
    mine = sum1[pl.ds(pl.multiple_of(j * GROUP, GROUP), GROUP), :]
    for k in range(C - 1):
        mine = mine + part2[k]
    both_ref[:GROUP, :] = jnp.where(my_lit[:GROUP], mine[:, :LANES], 0.0)
    both_ref[GROUP:owned_rows, :] = jnp.where(my_lit[GROUP:], mine[:, LANES:], 0.0)

    for copy in c2_copies:
        copy.wait_recv()
    ctotal = cpart2[0]
    for k in range(1, C):
        ctotal = ctotal + cpart2[k]
    result = jnp.where(c_lit, ctotal, 0.0)
    both_ref[owned_rows:, :] = result
    total_ref[0, 0] = jnp.sum(result)

    for copy in dat_copies + sup_copies + sum(row_copies, []) + c1_copies + h2_copies + c2_copies:
        copy.wait_send()


def per_device(R, C, fact_block, fact_offset, fact_date, revenue, supplier_words, date_words, candidates):
    rows = fact_offset.shape[0] // LANES
    cands = candidates.shape[0] // LANES
    tall_all = R * C * GROUP
    tall = min(tall_all, WIDE)
    span = C * GROUP
    f32, i32 = jnp.float32, jnp.int32
    dma = pltpu.SemaphoreType.DMA
    vmem = pl.BlockSpec(memory_space=pltpu.VMEM)
    both, total = pl.pallas_call(
        functools.partial(kernel, R, C),
        out_shape=(
            jax.ShapeDtypeStruct((SUP_DEV // LANES + cands, LANES), f32),
            jax.ShapeDtypeStruct((1, 1), f32),
        ),
        in_specs=[pl.BlockSpec(memory_space=pl.ANY)] * 7,
        out_specs=(vmem, pl.BlockSpec(memory_space=pltpu.SMEM)),
        scratch_shapes=[
            pltpu.VMEM((rows, LANES), i32),
            pltpu.VMEM((rows, LANES), i32),
            pltpu.VMEM((rows, LANES), i32),
            pltpu.VMEM((rows, LANES), revenue.dtype),
            pltpu.VMEM((cands, LANES), i32),
            dma((7,)),
            pltpu.VMEM((1, LANES), i32),
            pltpu.VMEM((rows, LANES), i32),
            pltpu.VMEM((rows, LANES), f32),
            pltpu.VMEM((rows, LANES), i32),
            pltpu.VMEM((rows, LANES), i32),
            pltpu.VMEM((tall, rows * LANES), jnp.bfloat16),
            pltpu.VMEM((WIDE, rows * LANES), jnp.bfloat16),
            pltpu.VMEM((span, rows * LANES), jnp.bfloat16),
            pltpu.VMEM((tall, cands * LANES), jnp.bfloat16),
            pltpu.VMEM((C, 1, date_words.shape[0]), i32),
            pltpu.VMEM((C, 1, supplier_words.shape[0]), i32),
            pltpu.VMEM((R - 1, rows, LANES), i32),
            pltpu.VMEM((R - 1, rows, LANES), i32),
            pltpu.VMEM((R - 1, rows, LANES), f32),
            pltpu.VMEM((span, WIDE), f32),
            pltpu.VMEM((C - 1, GROUP, WIDE), f32),
            pltpu.VMEM((cands, LANES), f32),
            pltpu.VMEM((R, cands, LANES), f32),
            pltpu.VMEM((cands, LANES), f32),
            pltpu.VMEM((C, cands, LANES), f32),
            dma((C - 1,)), dma((C - 1,)), dma((C - 1,)), dma((C - 1,)),
            dma((3, R - 1)), dma((3, R - 1)), dma((R - 1,)), dma((R - 1,)),
            dma((C - 1,)), dma((C - 1,)), dma((C - 1,)), dma((C - 1,)),
        ],
        compiler_params=pltpu.CompilerParams(collective_id=0, has_side_effects=True),
        name="revenue",
    )(
        fact_block.reshape(rows, LANES),
        fact_offset.reshape(rows, LANES),
        fact_date.reshape(rows, LANES),
        revenue.reshape(rows, LANES),
        candidates.reshape(cands, LANES),
        supplier_words,
        date_words.reshape(1, -1),
    )
    owned = both[: SUP_DEV // LANES].reshape(SUP_DEV)
    return owned, both[SUP_DEV // LANES :].reshape(candidates.shape), total.reshape(())


def solution(mesh):
    in_specs = (
        P(("row", "col"), None),
        P(("row", "col")),
        P(("row", "col")),
        P(("row", "col")),
        P("col"),
        P("col"),
        P(),
    )
    out_specs = (P(("row", "col")), P(), P())
    body = functools.partial(per_device, mesh.shape["row"], mesh.shape["col"])
    return jax.shard_map(body, mesh=mesh, in_specs=in_specs, out_specs=out_specs, check_vma=False)
```

```python
import functools

import jax
import jax.numpy as jnp
from jax import lax
from jax.experimental import pallas as pl
from jax.experimental.pallas import tpu as pltpu
from jax.sharding import PartitionSpec as P

SUP_DEV = 2048
LANES = 128
WIDE = 2 * LANES
GROUP = SUP_DEV // WIDE
BITS = 30
MESH = pl.DeviceIdType.MESH


def div_bits(x):
    return lax.shift_right_logical(x * 2185, 16)


def lookup(row, index):
    table = jnp.broadcast_to(row, index.shape)
    return jnp.take_along_axis(table, index, axis=1, mode="promise_in_bounds")


def kernel(
    rows_axis, cols_axis,
    block_in, offset_in, date_in, rev_in, cand_in, sup_in, dat_in,
    both_ref,
    block_ref, offset_ref, date_ref, rev_ref, cand_ref, load_sem, dat_row,
    ids, rev32, a_idx, b_idx, left, right, low_left, c_hot, dat_buf, sup_buf,
    peer_ids, peer_dates, peer_revs, sum1, part2,
    cpart, cpart1, csum1, cpart2,
    dat_send, dat_recv, sup_send, sup_recv, row_send, row_recv, c1_send, c1_recv,
    h2_send, h2_recv, c2_send, c2_recv,
):
    R, C = rows_axis, cols_axis
    i, j = lax.axis_index("row"), lax.axis_index("col")
    row_peers = [(lax.rem(i + k, R), j) for k in range(1, R)]
    col_peers = [(i, lax.rem(j + k, C)) for k in range(1, C)]
    n_rows = block_ref.shape[0]
    n_dates, n_words = dat_in.shape[1], sup_in.shape[0]
    per_block = n_words // R
    owned_rows = both_ref.shape[0] - cand_ref.shape[0]
    chunks = R * C * GROUP // left.shape[0]
    tall = left.shape[0]

    barrier = pltpu.get_barrier_semaphore()
    for peer in col_peers + row_peers:
        pl.semaphore_signal(barrier, inc=1, device_id=peer, device_id_type=MESH)

    pairs = [
        (offset_in, offset_ref), (block_in, block_ref), (date_in, date_ref), (rev_in, rev_ref),
        (cand_in, cand_ref), (dat_in, dat_buf.at[j]), (sup_in, sup_buf.at[j, 0]),
    ]
    loads = [pltpu.make_async_copy(src, dst, load_sem.at[n]) for n, (src, dst) in enumerate(pairs)]
    for load in loads:
        load.start()
    dat_row[...] = jnp.zeros_like(dat_row)
    for load in loads:
        load.wait()

    off = offset_ref[...]
    rev = rev_ref[...].astype(jnp.float32)
    ids[...] = block_ref[...] * SUP_DEV + off
    rev32[...] = rev
    a_idx[...] = block_ref[...] * GROUP + (lax.shift_right_logical(off, 7) & (GROUP - 1))
    b_idx[...] = lax.shift_right_logical(off, 10) * LANES + (off & (LANES - 1))

    pl.semaphore_wait(barrier, (C - 1) + (R - 1))

    def remote(src, dst, send, recv, peer):
        return pltpu.make_async_remote_copy(
            src_ref=src, dst_ref=dst, send_sem=send, recv_sem=recv, device_id=peer, device_id_type=MESH
        )

    dat_copies = [
        remote(dat_in, dat_buf.at[j], dat_send.at[k], dat_recv.at[k], col_peers[k]) for k in range(C - 1)
    ]
    sup_copies = [
        remote(sup_in, sup_buf.at[j, 0], sup_send.at[k], sup_recv.at[k], col_peers[k]) for k in range(C - 1)
    ]
    for copy in dat_copies:
        copy.start()
    row_copies = [
        [
            remote(src, dst.at[k], row_send.at[n, k], row_recv.at[n, k], row_peers[k])
            for n, (src, dst) in enumerate(((ids, peer_ids), (date_ref, peer_dates), (rev32, peer_revs)))
        ]
        for k in range(R - 1)
    ]
    for copies in row_copies:
        for copy in copies:
            copy.start()
    for copy in sup_copies:
        copy.start()

    iota_b = lax.broadcasted_iota(jnp.int32, (WIDE, LANES), 0)

    def build_right(columns):
        for r in range(n_rows):
            hit = iota_b == columns[r : r + 1, :]
            right[:, r * LANES : (r + 1) * LANES] = jnp.where(hit, 1.0, 0.0).astype(jnp.bfloat16)

    def build_left(where, lines, values):
        iota_a = lax.broadcasted_iota(jnp.int32, (where.shape[0], LANES), 0)
        for r in range(n_rows):
            hit = iota_a == lines[r : r + 1, :]
            where[:, r * LANES : (r + 1) * LANES] = jnp.where(hit, values[r : r + 1, :], 0.0).astype(jnp.bfloat16)

    def product(lines, columns):
        return lax.dot_general(lines, columns, (((1,), (1,)), ((), ())), preferred_element_type=jnp.float32)

    cand = cand_ref[...]
    c_owner = lax.shift_right_logical(cand, 11)
    c_off = cand & (SUP_DEV - 1)
    c_row = c_owner * GROUP + (lax.shift_right_logical(c_off, 7) & (GROUP - 1))
    c_col = lax.shift_right_logical(c_off, 10) * LANES + (c_off & (LANES - 1))
    groups = cand.shape[0]

    def build_hot(base):
        iota_c = lax.broadcasted_iota(jnp.int32, (tall, LANES), 0)
        for g in range(groups):
            hit = iota_c == c_row[g : g + 1, :] - base
            c_hot[:, g * LANES : (g + 1) * LANES] = jnp.where(hit, 1.0, 0.0).astype(jnp.bfloat16)

    if chunks == 1:
        build_hot(0)
        build_left(left, a_idx[...], rev)

    build_right(b_idx[...])

    for copy in dat_copies:
        copy.wait_recv()
    for c in range(C):
        dat_row[:, c * n_dates : (c + 1) * n_dates] = dat_buf[c]
    table = dat_row[...]

    def dated(day, values):
        day_word = div_bits(day)
        lit = lax.shift_right_logical(lookup(table, day_word), day - day_word * BITS) & 1
        return jnp.where(lit == 1, values, 0.0)

    lit_rows = dated(date_ref[...], jnp.ones_like(rev))
    for r in range(n_rows):
        part = right[:, r * LANES : (r + 1) * LANES]
        shown = jnp.broadcast_to(lit_rows[r : r + 1, :], part.shape).astype(jnp.bfloat16)
        right[:, r * LANES : (r + 1) * LANES] = part * shown

    def candidate_columns(base):
        if chunks > 1:
            build_left(left, a_idx[...] - base, rev)
        rest = product(right[...], left[...])
        found = jnp.zeros((WIDE, groups * LANES), jnp.float32)
        for _ in range(3):
            term = rest.astype(jnp.bfloat16)
            rest = rest - term.astype(jnp.float32)
            found = found + jnp.dot(term, c_hot[...], preferred_element_type=jnp.float32)
        return found

    if chunks == 1:
        found = candidate_columns(0)
    else:

        def body(c, acc):
            build_hot(c * tall)
            return acc + candidate_columns(c * tall)

        found = lax.fori_loop(0, chunks, body, jnp.zeros((WIDE, groups * LANES), jnp.float32))
    picked = []
    for g in range(groups):
        hit = iota_b == c_col[g : g + 1, :]
        picked.append(jnp.sum(jnp.where(hit, found[:, g * LANES : (g + 1) * LANES], 0.0), axis=0, keepdims=True))
    picked = jnp.concatenate(picked, axis=0)
    cpart[...] = picked
    cpart1[i] = picked
    c1_copies = [
        remote(cpart, cpart1.at[i], c1_send.at[k], c1_recv.at[k], row_peers[k]) for k in range(R - 1)
    ]
    for copy in c1_copies:
        copy.start()

    span = C * GROUP
    if chunks == 1:
        total = product(left[pl.ds(pl.multiple_of(i * span, span), span), :], right[...])
    else:
        build_left(low_left, a_idx[...] - i * span, rev)
        total = product(low_left[...], right[...])
    for k in range(R - 1):
        for copy in row_copies[k]:
            copy.wait_recv()
        peer_id = peer_ids[k]
        line = lax.shift_right_logical(peer_id, 11) * GROUP + (lax.shift_right_logical(peer_id, 7) & (GROUP - 1))
        build_right((lax.shift_right_logical(peer_id, 10) & 1) * LANES + (peer_id & (LANES - 1)))
        build_left(low_left, line - i * span, dated(peer_dates[k], peer_revs[k]))
        total = total + product(low_left[...], right[...])
    sum1[...] = total
    h2_copies = [
        remote(
            sum1.at[pl.ds(pl.multiple_of(col_peers[k][1] * GROUP, GROUP), GROUP), :],
            part2.at[k], h2_send.at[k], h2_recv.at[k], col_peers[k],
        )
        for k in range(C - 1)
    ]
    for copy in h2_copies:
        copy.start()

    for copy in c1_copies:
        copy.wait_recv()
    ctotal = cpart1[0]
    for k in range(1, R):
        ctotal = ctotal + cpart1[k]
    csum1[...] = ctotal
    cpart2[j] = ctotal
    c2_copies = [
        remote(csum1, cpart2.at[j], c2_send.at[k], c2_recv.at[k], col_peers[k]) for k in range(C - 1)
    ]
    for copy in c2_copies:
        copy.start()

    for copy in sup_copies:
        copy.wait_recv()

    full = n_words // LANES

    def words_at(source, flat):
        word = lookup(sup_buf[source, :, n_words - LANES :], jnp.maximum(flat - (n_words - LANES), 0))
        for t in range(full):
            near = (flat >= t * LANES) & (flat < (t + 1) * LANES)
            word = jnp.where(near, lookup(sup_buf[source, :, t * LANES : (t + 1) * LANES], flat & (LANES - 1)), word)
        return word

    c_word = div_bits(c_off)
    c_bit = c_off - c_word * BITS
    c_source = lax.div(c_owner, R)
    c_flat = (c_owner - c_source * R) * per_block + c_word

    def word_of(source, acc):
        return jnp.where(c_source == source, words_at(source, c_flat), acc)

    c_words = lax.fori_loop(0, C, word_of, jnp.zeros(cand.shape, jnp.int32))
    c_lit = (lax.shift_right_logical(c_words, c_bit) & 1) == 1

    me = i * C + j
    shape = (owned_rows, LANES)
    spot = lax.broadcasted_iota(jnp.int32, shape, 0) * LANES + lax.broadcasted_iota(jnp.int32, shape, 1)
    spot_word = div_bits(spot)
    my_words = words_at(me // R, lax.rem(me, R) * per_block + spot_word)
    my_lit = (lax.shift_right_logical(my_words, spot - spot_word * BITS) & 1) == 1

    for copy in h2_copies:
        copy.wait_recv()
    mine = sum1[pl.ds(pl.multiple_of(j * GROUP, GROUP), GROUP), :]
    for k in range(C - 1):
        mine = mine + part2[k]
    both_ref[:GROUP, :] = jnp.where(my_lit[:GROUP], mine[:, :LANES], 0.0)
    both_ref[GROUP:owned_rows, :] = jnp.where(my_lit[GROUP:], mine[:, LANES:], 0.0)

    for copy in c2_copies:
        copy.wait_recv()
    ctotal = cpart2[0]
    for k in range(1, C):
        ctotal = ctotal + cpart2[k]
    result = jnp.where(c_lit, ctotal, 0.0)
    both_ref[owned_rows:, :] = result

    for copy in dat_copies + sup_copies + sum(row_copies, []) + c1_copies + h2_copies + c2_copies:
        copy.wait_send()


def finish(both_ref, owned_ref, cand_out_ref, total_ref):
    owned_rows = owned_ref.shape[0]
    owned_ref[...] = both_ref[:owned_rows, :]
    found = both_ref[owned_rows:, :]
    cand_out_ref[...] = found
    total_ref[0, 0] = jnp.sum(found)


def per_device(R, C, fact_block, fact_offset, fact_date, revenue, supplier_words, date_words, candidates):
    rows = fact_offset.shape[0] // LANES
    cands = candidates.shape[0] // LANES
    tall_all = R * C * GROUP
    tall = min(tall_all, WIDE)
    span = C * GROUP
    f32, i32 = jnp.float32, jnp.int32
    dma = pltpu.SemaphoreType.DMA
    vmem = pl.BlockSpec(memory_space=pltpu.VMEM)
    both = pl.pallas_call(
        functools.partial(kernel, R, C),
        out_shape=jax.ShapeDtypeStruct((SUP_DEV // LANES + cands, LANES), f32),
        in_specs=[pl.BlockSpec(memory_space=pl.ANY)] * 7,
        out_specs=vmem,
        scratch_shapes=[
            pltpu.VMEM((rows, LANES), i32),
            pltpu.VMEM((rows, LANES), i32),
            pltpu.VMEM((rows, LANES), i32),
            pltpu.VMEM((rows, LANES), revenue.dtype),
            pltpu.VMEM((cands, LANES), i32),
            dma((7,)),
            pltpu.VMEM((1, LANES), i32),
            pltpu.VMEM((rows, LANES), i32),
            pltpu.VMEM((rows, LANES), f32),
            pltpu.VMEM((rows, LANES), i32),
            pltpu.VMEM((rows, LANES), i32),
            pltpu.VMEM((tall, rows * LANES), jnp.bfloat16),
            pltpu.VMEM((WIDE, rows * LANES), jnp.bfloat16),
            pltpu.VMEM((span, rows * LANES), jnp.bfloat16),
            pltpu.VMEM((tall, cands * LANES), jnp.bfloat16),
            pltpu.VMEM((C, 1, date_words.shape[0]), i32),
            pltpu.VMEM((C, 1, supplier_words.shape[0]), i32),
            pltpu.VMEM((R - 1, rows, LANES), i32),
            pltpu.VMEM((R - 1, rows, LANES), i32),
            pltpu.VMEM((R - 1, rows, LANES), f32),
            pltpu.VMEM((span, WIDE), f32),
            pltpu.VMEM((C - 1, GROUP, WIDE), f32),
            pltpu.VMEM((cands, LANES), f32),
            pltpu.VMEM((R, cands, LANES), f32),
            pltpu.VMEM((cands, LANES), f32),
            pltpu.VMEM((C, cands, LANES), f32),
            dma((C - 1,)), dma((C - 1,)), dma((C - 1,)), dma((C - 1,)),
            dma((3, R - 1)), dma((3, R - 1)), dma((R - 1,)), dma((R - 1,)),
            dma((C - 1,)), dma((C - 1,)), dma((C - 1,)), dma((C - 1,)),
        ],
        compiler_params=pltpu.CompilerParams(collective_id=0, has_side_effects=True),
        name="revenue",
    )(
        fact_block.reshape(rows, LANES),
        fact_offset.reshape(rows, LANES),
        fact_date.reshape(rows, LANES),
        revenue.reshape(rows, LANES),
        candidates.reshape(cands, LANES),
        supplier_words,
        date_words.reshape(1, -1),
    )
    owned, found, total = pl.pallas_call(
        finish,
        out_shape=(
            jax.ShapeDtypeStruct((SUP_DEV // LANES, LANES), f32),
            jax.ShapeDtypeStruct((cands, LANES), f32),
            jax.ShapeDtypeStruct((1, 1), f32),
        ),
        in_specs=[vmem],
        out_specs=(vmem, vmem, pl.BlockSpec(memory_space=pltpu.SMEM)),
        name="finish",
    )(both)
    return owned.reshape(SUP_DEV), found.reshape(candidates.shape), total.reshape(())


def solution(mesh):
    in_specs = (
        P(("row", "col"), None),
        P(("row", "col")),
        P(("row", "col")),
        P(("row", "col")),
        P("col"),
        P("col"),
        P(),
    )
    out_specs = (P(("row", "col")), P(), P())
    body = functools.partial(per_device, mesh.shape["row"], mesh.shape["col"])
    return jax.shard_map(body, mesh=mesh, in_specs=in_specs, out_specs=out_specs, check_vma=False)
```
